128 devices in a mesh: sub: 16 (over x, y), row: 8 (over z, core).
Axes of the slice: x: 4, y: 4, z: 4, core: 2. Of those that a mesh axis runs over, the one named last changes fastest.
Arguments:
- sigma_top: float32 [6144, 6144], P('row', 'sub'), may hold values from -2 to 4, as said below
- coupling: float32 [16, 6144, 768], P('sub', 'row'), may hold values from -0.16 to 0.16
- child_inverse: float32 [16, 768, 768], P('sub', 'row'), may hold values from -1 to 10, as said below
- tile_mask: int32 [16, 24], P('sub'), may hold values 0 or 1
- obs_node: int32 [32768], P(('sub', 'row')), may hold values from 0 to 12287
- obs_noise: float32 [32768], P(('sub', 'row')), may hold values from 0.05 to 2
Outputs:
- sep_child: float32 [16, 6144, 768], P('sub', 'row')
- child_block: float32 [16, 768, 768], P('sub', 'row')
- loo_var: float32 [32768], P(('sub', 'row'))
The draws below stay inside these ranges and needn't reach their ends.
Inputs may be any that keep to these rules, and one draw needn't show every extreme that they name: sigma_top is exactly symmetric. Each child_inverse[c] is exactly symmetric.
All inputs are finite; a program needn't handle non-finite values. No bound on the sum of `tile_mask` on one device may be relied on, other than what follows from the above.
Results may differ from the reference program's by a relative error of at most 0.000073.
Values sent between devices are 32-bit elements; how exact they have to be, the bound alone decides.
No kernel may reach another device: no remote copies, remote signals or barrier semaphores. Data moves between devices by JAX's collectives and lax.ppermute only.
A program may use at most 128 MiB of HBM per device.

```python
import math
import jax
import jax.numpy as jnp
from jax import lax

TILE = 256
ST = 24
CW = 768
SEP = 6144
CHILDREN = 16
NOBS = 32768


def draw_sigma_top(key, part):
    size_all = ST * TILE
    key_a, key_b = jax.random.split(jax.random.fold_in(key, 11), 2)
    raw = jnp.clip(jax.random.normal(key_a, (size_all, size_all), jnp.float32), -4.0, 4.0)
    coeff = 0.4 / size_all ** 0.5
    sym = (raw + raw.T) * coeff
    diag_vals = jax.random.uniform(key_b, (size_all,), jnp.float32, 1.5, 2.5)
    ident = lax_iota_eq(size_all).astype(jnp.float32)
    return sym * (1.0 - ident) + ident * diag_vals[:, None]


def lax_iota_eq(size_all):
    idx = jnp.arange(size_all, dtype=jnp.int32)
    return idx[:, None] == idx[None, :]


def draw_child_inverse(key, part):
    key_a, key_b = jax.random.split(jax.random.fold_in(key, 23), 2)
    raw = jnp.clip(jax.random.normal(key_a, (CHILDREN, CW, CW), jnp.float32), -4.0, 4.0)
    sym = (raw + jnp.swapaxes(raw, 1, 2)) * (0.5 / CW ** 0.5)
    diag_vals = jax.random.uniform(key_b, (CHILDREN, CW), jnp.float32, 6.0, 10.0)
    ident = lax_iota_eq(CW).astype(jnp.float32)
    return sym * (1.0 - ident)[None] + ident[None] * diag_vals[:, :, None]


def touch_ends(entries, own_key, smallest, top_value):
    shape = entries.shape
    place = [jax.random.randint(jax.random.fold_in(own_key, axis), (), 0, shape[axis]) for axis in range(len(shape))]
    entries = entries.at[tuple(place)].set(smallest)
    longest = shape.index(max(shape))
    place[longest] = (place[longest] + 1) % shape[longest]
    return entries.at[tuple(place)].set(top_value)


def steps_of(rng, dims, shards, smallest, high):
    def one(dim, parts):
        heights = jax.random.uniform(jax.random.fold_in(jax.random.fold_in(rng, 6), dim), (parts,), jnp.float32, smallest / len(shards), high / len(shards))
        return jnp.repeat(jnp.exp(heights), dims[dim] // parts).reshape((-1,) + (1,) * (len(dims) - dim - 1))

    factor_of = one(*shards[0])
    for cut in shards[1:]:
        factor_of = factor_of * one(*cut)
    return factor_of


def scatter_about(stream_key, shape, scale, reach, pieces=(), held_as=jnp.bfloat16):
    drawn = jax.random.normal(stream_key, shape, jnp.float32) * scale
    if len(pieces) > 0:
        drawn = steps_of(stream_key, shape, pieces, -0.22, 0.18) * drawn
    return jnp.clip(drawn, min=-reach, max=reach).astype(held_as)


def setup_inputs(seed: int = 0) -> dict:
    key_list = jax.random.split(jax.random.key(seed), 7)
    return {
        "sigma_top": draw_sigma_top(jax.random.fold_in(key_list[6], 71), 0),
        "coupling": scatter_about(key_list[1], (CHILDREN, SEP, CW), 0.025, 0.16, ((0, 16), (1, 8)), jnp.float32),
        "child_inverse": draw_child_inverse(jax.random.fold_in(key_list[6], 71), 0),
        "tile_mask": touch_ends((jax.random.randint(key_list[3], (CHILDREN, ST), 0, 8) < 5).astype(jnp.int32), jax.random.fold_in(key_list[3], 1), 0, 1),
        "obs_node": touch_ends(jax.random.randint(key_list[4], (NOBS,), 0, CHILDREN * CW), jax.random.fold_in(key_list[4], 1), 0, (CHILDREN * CW) - 1).astype(jnp.int32),
        "obs_noise": jnp.clip(jnp.exp(math.log(2.0) - 3.6888794 * jax.random.uniform(key_list[5], (NOBS,), jnp.float32) ** steps_of(key_list[5], (NOBS,), ((0, 128),), -0.2, 0.2)), 0.05, 2.0),
    }


def reference(sigma_top, coupling, child_inverse, tile_mask, obs_node, obs_noise):
    highest = lax.Precision.HIGHEST
    row_mask = jnp.repeat(tile_mask, TILE, axis=1).astype(jnp.float32)
    masked = coupling * row_mask[:, :, None]

    def per_child(pair):
        coupled, inverse = pair
        product = jnp.dot(sigma_top, coupled, precision=highest, preferred_element_type=jnp.float32)
        sep_part = -product
        update = jnp.dot(coupled.T, sep_part, precision=highest, preferred_element_type=jnp.float32)
        return sep_part, inverse - update

    sep_child, child_block = lax.map(per_child, (masked, child_inverse))
    variances = jnp.diagonal(child_block, axis1=1, axis2=2).reshape(-1)
    loo_var = variances[obs_node] + obs_noise
    return sep_child, child_block, loo_var
```

```python
import jax
import jax.numpy as jnp
from jax import lax
from jax.experimental import pallas as pl
from jax.experimental.pallas import tpu as pltpu
from jax.sharding import PartitionSpec as P

AXES = ("sub", "row")
BOTH = jnp.bfloat16


def place(x, y, z, c):
    return (x % 4) * 32 + (y % 4) * 8 + (z % 4) * 2 + c % 2


def send(value, dx=0, dy=0, dz=0, dc=0):
    pairs = [
        (place(x, y, z, c), place(x + dx, y + dy, z + dz, c + dc))
        for x in range(4)
        for y in range(4)
        for z in range(4)
        for c in range(2)
    ]
    return lax.ppermute(value, AXES, pairs)


def split(value):
    high = value.astype(BOTH)
    low = (value - high.astype(jnp.float32)).astype(BOTH)
    return high, low


def dot3(a, b, dims):
    a_high, a_low = a
    b_high, b_low = b
    one = lambda u, v: lax.dot_general(u, v, (dims, ((), ())), preferred_element_type=jnp.float32)
    return one(a_high, b_high) + (one(a_low, b_high) + one(a_high, b_low))


ROWS = ((1,), (0,))
COLS = ((0,), (0,))


def pair_loop(pairs, sources, where, mask, coupling_all, sums, s_buf, m_buf, m_index, s_sem, m_sem):
    x = where[0]
    y = where[1]
    count = len(pairs)
    half_of = count // 2

    def start(q, slot):
        source, unit, first, second = pairs[q]
        for part, (dx, dy) in enumerate((first, second)):
            block = ((x + dx) & 3) * 4 + ((y + dy) & 3)
            m_index[slot, part] = block
            pltpu.make_async_copy(
                sources[source].at[unit + part], s_buf.at[slot, :, pl.ds(part * 384, 384)], s_sem.at[slot, part]
            ).start()
            pltpu.make_async_copy(
                coupling_all.at[block], m_buf.at[slot, pl.ds(part * 384, 384), :], m_sem.at[slot, part]
            ).start()

    start(0, 0)

    def step(p, carry):
        slot = p % 2
        for q in range(1, count):

            @pl.when(p + 1 == q)
            def _():
                start(q, 1 - slot)

        for part in range(2):
            pltpu.make_async_copy(
                sources[0].at[0], s_buf.at[slot, :, pl.ds(part * 384, 384)], s_sem.at[slot, part]
            ).wait()
            pltpu.make_async_copy(
                coupling_all.at[0], m_buf.at[slot, pl.ds(part * 384, 384), :], m_sem.at[slot, part]
            ).wait()
        pieces = []
        for part in range(2):
            for third in range(3):
                tile = (m_index[slot, part] * 3 + third) >> 1
                factor = mask[tile].astype(jnp.float32)
                pieces.append(m_buf[slot, pl.ds(part * 384 + third * 128, 128), :] * factor)
        m_value = jnp.concatenate(pieces, axis=0)
        part_sum = dot3(split(s_buf[slot]), split(m_value), ROWS)
        row_half = p // half_of
        sums[row_half] = sums[row_half] + part_sum
        return carry

    lax.fori_loop(0, count, step, 0)


ORDER = (0, -1, 1, 2)


def first_pairs():
    out = []
    for k, dy in enumerate((0, -1, 1)):
        for unit in (0, 2):
            out.append((k, unit, (ORDER[unit], dy), (ORDER[unit + 1], dy)))
    for k, dx in enumerate((0, -1, 1)):
        for unit in (0, 2):
            out.append((3 + k, unit, (dx, ORDER[unit]), (dx, ORDER[unit + 1])))
    return out


def last_pairs():
    return [
        (0, 0, (ORDER[0], 2), (ORDER[1], 2)),
        (1, 0, (ORDER[2], 2), (ORDER[3], 2)),
        (2, 0, (2, ORDER[0]), (2, ORDER[1])),
        (3, 0, (2, ORDER[2]), (2, ORDER[3])),
    ]


def first_body(where, mask, coupling_all, *rest):
    sources, sums, scratch = rest[:6], rest[6], rest[7:]
    sums[...] = jnp.zeros_like(sums)
    pair_loop(first_pairs(), sources, where, mask, coupling_all, sums, *scratch)


def last_body(where, mask, coupling_all, s0, s1, s2, s3, before, own, diag_here, sep, mine, other, part_var, *scratch):
    sums, scratch = scratch[0], scratch[1:]
    sums[...] = before[...]
    pair_loop(last_pairs(), (s0, s1, s2, s3), where, mask, coupling_all, sums, *scratch)
    row = where[2]
    core = where[3]
    product = jnp.concatenate([sums[0], sums[1]], axis=0)
    sep[...] = -product
    tiles = [own[pl.ds(k * 256, 256), :] * mask[row * 3 + k].astype(jnp.float32) for k in range(3)]
    own_value = jnp.concatenate(tiles, axis=0)
    part_var[...] = diag_here[...] + jnp.sum(own_value * product, axis=0, keepdims=True)
    update = dot3(split(own_value), split(product), COLS)
    for zz in range(4):
        lower = update[zz * 192 : zz * 192 + 96]
        upper = update[zz * 192 + 96 : zz * 192 + 192]

        @pl.when(core == 0)
        def _():
            mine[zz] = lower
            other[zz] = upper

        @pl.when(core != 0)
        def _():
            mine[zz] = upper
            other[zz] = lower


ANY = pl.BlockSpec(memory_space=pl.ANY)
SMEM = pl.BlockSpec(memory_space=pltpu.SMEM)
VMEM = pl.BlockSpec(memory_space=pltpu.VMEM)


def buffers():
    return [
        pltpu.VMEM((2, 384, 768), jnp.float32),
        pltpu.VMEM((2, 768, 768), jnp.float32),
        pltpu.SMEM((2, 2), jnp.int32),
        pltpu.SemaphoreType.DMA((2, 2)),
        pltpu.SemaphoreType.DMA((2, 2)),
    ]


def shape(*dims):
    return jax.ShapeDtypeStruct(dims, jnp.float32)


def local(sigma_top, coupling, child_inverse, tile_mask, obs_node, obs_noise):
    sub = lax.axis_index("sub")
    row = lax.axis_index("row")
    x, y, z, core = sub // 4, sub % 4, row // 2, row % 2
    where = jnp.stack([x, y, row, core]).astype(jnp.int32)
    mask = tile_mask[0]
    coupling_all = lax.all_gather(coupling[0], "row", axis=0, tiled=True).reshape(16, 384, 768)

    a = sigma_top[:384]
    b = sigma_top[384:]
    a_minus = send(a, dx=1)
    b_minus = send(b, dy=1)
    a_plus = send(a, dx=-1)
    b_plus = send(b, dy=-1)
    a_two = jnp.concatenate([send(a_minus[:192], dx=1), send(a_plus[192:], dx=-1)], axis=0)
    b_two = jnp.concatenate([send(b_minus[:192], dy=1), send(b_plus[192:], dy=-1)], axis=0)
    a_line = jnp.stack([a, a_minus, a_plus, a_two])
    b_line = jnp.stack([b, b_minus, b_plus, b_two])
    a_line_minus = send(a_line, dy=1)
    b_line_minus = send(b_line, dx=1)
    a_line_plus = send(a_line, dy=-1)
    b_line_plus = send(b_line, dx=-1)
    a_far0 = send(a_line_minus[:2], dy=1)
    b_far0 = send(b_line_minus[:2], dx=1)
    a_far1 = send(a_line_plus[2:], dy=-1)
    b_far1 = send(b_line_plus[2:], dx=-1)

    sums = pl.pallas_call(
        first_body,
        out_shape=shape(2, 384, 768),
        in_specs=[SMEM, SMEM] + [ANY] * 7,
        out_specs=VMEM,
        scratch_shapes=buffers(),
        compiler_params=pltpu.CompilerParams(vmem_limit_bytes=48 << 20),
        cost_estimate=pl.CostEstimate(flops=16_000_000_000, bytes_accessed=45_000_000, transcendentals=0),
        name="first_pairs",
    )(where, mask, coupling_all, a_line, a_line_minus, a_line_plus, b_line, b_line_minus, b_line_plus)

    inverse = child_inverse[0]
    column = lax.broadcasted_iota(jnp.int32, (96, 768), 1)
    line = lax.broadcasted_iota(jnp.int32, (96, 768), 0) + row * 96
    diag_here = jnp.sum(jnp.where(column == line, inverse, 0.0), axis=0, keepdims=True)
    sep, mine, other, part_var = pl.pallas_call(
        last_body,
        out_shape=(shape(768, 768), shape(4, 96, 768), shape(4, 96, 768), shape(1, 768)),
        in_specs=[SMEM, SMEM] + [ANY] * 5 + [VMEM] * 3,
        out_specs=(VMEM, VMEM, VMEM, VMEM),
        scratch_shapes=[pltpu.VMEM((2, 384, 768), jnp.float32)] + buffers(),
        compiler_params=pltpu.CompilerParams(vmem_limit_bytes=56 << 20),
        cost_estimate=pl.CostEstimate(flops=8_000_000_000, bytes_accessed=25_000_000, transcendentals=0),
        name="last_pairs",
    )(where, mask, coupling_all, a_far0, a_far1, b_far0, b_far1, sums, coupling[0], diag_here)

    half_sum = mine + send(other, dc=1)
    part = part_var + send(part_var, dc=1)
    toward = lambda dz: lax.dynamic_index_in_dim(half_sum, (z + dz) % 4, 0, False)
    part = part + send(part, dz=1) + send(part, dz=-1) + send(part, dz=2)
    block_here = inverse + (toward(0) + send(toward(1), dz=1) + send(toward(-1), dz=-1) + send(toward(2), dz=2))
    by_y = jnp.concatenate([part, send(part, dy=-1), send(part, dy=2), send(part, dy=1)], axis=0)
    by_xy = jnp.stack([by_y, send(by_y, dx=-1), send(by_y, dx=2), send(by_y, dx=1)])
    child = obs_node // 768
    far_x = (child // 4 - x) % 4
    far_y = (child % 4 - y) % 4
    index = (far_x * 4 + far_y) * 768 + obs_node % 768
    loo_var = by_xy.reshape(-1)[index] + obs_noise
    return sep[None], block_here[None], loo_var


def solution(mesh):
    placed = (
        P("row", "sub"),
        P("sub", "row", None),
        P("sub", "row", None),
        P("sub", None),
        P(("sub", "row")),
        P(("sub", "row")),
    )
    return jax.shard_map(
        local,
        mesh=mesh,
        in_specs=placed,
        out_specs=(P("sub", "row", None), P("sub", "row", None), P(("sub", "row"))),
        check_vma=False,
    )
```

```python
import jax
import jax.numpy as jnp
from jax import lax
from jax.experimental import pallas as pl
from jax.experimental.pallas import tpu as pltpu
from jax.sharding import PartitionSpec as P

AXES = ("sub", "row")
SHORT = jnp.bfloat16
FULL = jnp.float32


def place(x, y, z, c):
    return (x % 4) * 32 + (y % 4) * 8 + (z % 4) * 2 + c % 2


def send(value, dx=0, dy=0, dz=0, dc=0, turn=False):
    pairs = []
    for x in range(4):
        for y in range(4):
            for z in range(4):
                for c in range(2):
                    way = -1 if turn and c else 1
                    pairs.append((place(x, y, z, c), place(x + way * dx, y + way * dy, z + way * dz, c + dc)))
    return lax.ppermute(value, AXES, pairs)


def ring(value, axis, step, name):
    with jax.named_scope(name):
        return send(value, turn=True, **{"d" + axis: step})


def swap(value, name="swap"):
    with jax.named_scope(name):
        return send(value, dc=1)


def after(value, *earlier):
    return lax.optimization_barrier((value,) + earlier)[0]


def split(value):
    high = value.astype(SHORT)
    low = (value - high.astype(FULL)).astype(SHORT)
    return high, low


def dot3(a, b, dims):
    a_high, a_low = a
    b_high, b_low = b
    one = lambda u, v: lax.dot_general(u, v, (dims, ((), ())), preferred_element_type=FULL)
    return one(a_high, b_high) + (one(a_low, b_high) + one(a_high, b_low))


ROWS = ((1,), (0,))
COLS = ((0,), (0,))

LINES = ("a0", "a1", "a2", "a3", "b0", "b1", "b2", "b3")


def work_table(x, y, z, core, way):
    unit = jnp.arange(32, dtype=jnp.int32)
    group, line, spot = unit // 16, unit // 4 % 4, unit % 4
    step = lambda k: jnp.where(k == 3, 2, jnp.where(k == 0, 0, 2 * k - 3))
    x_step = jnp.where(group == 0, step(spot), step(line))
    y_step = jnp.where(group == 0, step(line), step(spot))
    at_x = (x + way * x_step) & 3
    at_y = (y + way * y_step) & 3
    far = ((at_x - z) * way) & 3
    other = (at_y >> 1) ^ core
    late = (far == 3) | ((far == 2) & (other == 1))
    array = jnp.where(far == 0, other, jnp.where(far == 1, 2 + other, jnp.where(far == 2, 3 + other, 4 + other)))
    begin = jnp.where((far == 2), 2, 0)
    half = array * 4 + begin + (at_y & 1)
    rank = jnp.where(line == 3, 2, late.astype(jnp.int32))
    early = jnp.sum((rank.reshape(2, 16) == 0).astype(jnp.int32), axis=1)
    key = (group * 3 + rank) * 32 + unit
    order = jnp.sum((key[None, :] < key[:, None]).astype(jnp.int32), axis=1)
    here = (order[None, :] == unit[:, None]).astype(jnp.int32)
    pick = lambda v: jnp.sum(here * v[None, :], axis=1)
    return jnp.stack([pick(unit), pick(half), pick(at_x * 4 + at_y)]), early


def pair_loop(begin, end, refs, table, mask, sums, s_buf, m_buf, spot, s_sem, m_sem):
    first_group = end[0] - begin[0]
    count = first_group + end[1] - begin[1]

    def start(q, slot):
        group = jnp.where(q < first_group, 0, 1)
        pair = jnp.where(q < first_group, begin[0] + q, begin[1] + q - first_group)
        spot[slot, 2] = group
        for part in range(2):
            entry = group * 16 + pair * 2 + part
            unit = table[0, entry]
            half = table[1, entry]
            spot[slot, part] = table[2, entry]
            s_target = s_buf.at[slot, :, pl.ds(part * 384, 384)]
            m_target = m_buf.at[slot, pl.ds(part * 384, 384), :]
            for number, name in enumerate(LINES):
                if name in refs:

                    @pl.when(unit >> 2 == number)
                    def _():
                        pltpu.make_async_copy(refs[name].at[unit & 3], s_target, s_sem.at[slot, part]).start()

            for number, name in enumerate(("own", "sib", "za", "zb", "zs", "zt")):
                if name in refs:

                    @pl.when(half >> 2 == number)
                    def _():
                        pltpu.make_async_copy(refs[name].at[half & 3], m_target, m_sem.at[slot, part]).start()

    def finish(slot):
        for part in range(2):
            target = s_buf.at[slot, :, pl.ds(part * 384, 384)]
            pltpu.make_async_copy(refs["a0"].at[0], target, s_sem.at[slot, part]).wait()
            target = m_buf.at[slot, pl.ds(part * 384, 384), :]
            pltpu.make_async_copy(refs["own"].at[0], target, m_sem.at[slot, part]).wait()
        pieces = []
        for part in range(2):
            block = spot[slot, part]
            for third in range(3):
                factor = mask[(block * 3 + third) >> 1].astype(FULL)
                pieces.append(m_buf[slot, pl.ds(part * 384 + third * 128, 128), :] * factor)
        part_sum = dot3(split(s_buf[slot]), split(jnp.concatenate(pieces, axis=0)), ROWS)
        group = spot[slot, 2]
        sums[group] = sums[group] + part_sum

    def step(p, carry):
        @pl.when(p < count)
        def _():
            start(p, p % 2)

        @pl.when(p > 0)
        def _():
            finish((p + 1) % 2)

        return carry

    lax.fori_loop(0, jnp.where(count > 0, count + 1, 0), step, 0)


HBM = pl.BlockSpec(memory_space=pl.ANY)
SMEM = pl.BlockSpec(memory_space=pltpu.SMEM)
VMEM = pl.BlockSpec(memory_space=pltpu.VMEM)


def buffers():
    return [
        pltpu.VMEM((2, 384, 768), FULL),
        pltpu.VMEM((2, 768, 768), FULL),
        pltpu.SMEM((2, 3), jnp.int32),
        pltpu.SemaphoreType.DMA((2, 2)),
        pltpu.SemaphoreType.DMA((2, 2)),
    ]


def shape(*dims):
    return jax.ShapeDtypeStruct(dims, FULL)


def cost(pairs):
    return pl.CostEstimate(flops=1_400_000_000 * pairs, bytes_accessed=3_600_000 * pairs, transcendentals=0)


def products(turn, where, mask, table, pieces, before, name):
    names = list(pieces)
    first = [] if before is None else [before]

    def body(where_ref, mask_ref, table_ref, *rest):
        refs = dict(zip(names, rest))
        rest = rest[len(names) :]
        if first:
            start, sums = rest[0], rest[1]
            sums[...] = start[...]
            rest = rest[2:]
        else:
            sums = rest[0]
            sums[...] = jnp.zeros_like(sums)
            rest = rest[1:]
        early = (where_ref[6] // 2, where_ref[7] // 2)
        begin, end = ((0, 0), early) if turn == 0 else (early, (6, 6))
        pair_loop(begin, end, refs, table_ref, mask_ref, sums, *rest)

    return pl.pallas_call(
        body,
        out_shape=shape(2, 384, 768),
        in_specs=[SMEM, SMEM, SMEM] + [HBM] * len(names) + [VMEM] * len(first),
        out_specs=VMEM,
        scratch_shapes=buffers(),
        compiler_params=pltpu.CompilerParams(vmem_limit_bytes=54 << 20),
        cost_estimate=cost(6),
        name=name,
    )(where, mask, table, *pieces.values(), *first)


def last_products(where, mask, table, pieces, before, own, diag_here):
    names = list(pieces)

    def body(where_ref, mask_ref, table_ref, *rest):
        refs = dict(zip(names, rest))
        start, own_ref, diag_ref, sep, part_var, sums = rest[len(names) : len(names) + 6]
        sums[...] = start[...]
        pair_loop((6, 6), (8, 8), refs, table_ref, mask_ref, sums, *rest[len(names) + 6 :])
        row = where_ref[5]
        total = diag_ref[...]
        for k in range(3):
            factor = mask_ref[row * 3 + k].astype(FULL)
            if k == 1:
                piece = jnp.concatenate([sums[0, 256:384], sums[1, 0:128]], axis=0)
            else:
                piece = sums[k // 2, pl.ds(128 if k == 2 else 0, 256), :]
            sep[pl.ds(k * 256, 256), :] = -piece
            total = total + factor * jnp.sum(own_ref[pl.ds(k * 256, 256), :] * piece, axis=0, keepdims=True)
        part_var[...] = total

    return pl.pallas_call(
        body,
        out_shape=(shape(768, 768), shape(1, 768)),
        in_specs=[SMEM, SMEM, SMEM] + [HBM] * len(names) + [VMEM] * 3,
        out_specs=(VMEM, VMEM),
        scratch_shapes=[pltpu.VMEM((2, 384, 768), FULL)] + buffers(),
        compiler_params=pltpu.CompilerParams(vmem_limit_bytes=54 << 20),
        cost_estimate=cost(4),
        name="last_products",
    )(where, mask, table, *pieces.values(), before, own, diag_here)


def update_body(where, mask, own, sep, mine, other):
    row = where[5]
    core = where[3]
    tiles = [own[pl.ds(k * 256, 256), :] * mask[row * 3 + k].astype(FULL) for k in range(3)]
    update = -dot3(split(jnp.concatenate(tiles, axis=0)), split(sep[...]), COLS)
    for zz in range(4):
        lower = update[zz * 192 : zz * 192 + 96]
        upper = update[zz * 192 + 96 : zz * 192 + 192]

        @pl.when(core == 0)
        def _():
            mine[zz] = lower
            other[zz] = upper

        @pl.when(core != 0)
        def _():
            mine[zz] = upper
            other[zz] = lower


def local(sigma_top, coupling, child_inverse, tile_mask, obs_node, obs_noise):
    sub = lax.axis_index("sub")
    row = lax.axis_index("row")
    x, y, z, core = sub // 4, sub % 4, row // 2, row % 2
    way = 1 - 2 * core
    table, early = work_table(x, y, z, core, way)
    where = jnp.concatenate([jnp.stack([x, y, z, core, way, row]).astype(jnp.int32), early])
    mask = tile_mask[0]

    a = sigma_top[:384]
    b = sigma_top[384:]
    m = coupling[0].reshape(2, 384, 768)
    xm, ym = ring(a, "x", 1, "p1"), ring(b, "y", 1, "p1")
    xp, yp = ring(a, "x", -1, "p1"), ring(b, "y", -1, "p1")
    za = ring(m, "z", -1, "p1z")

    one = (xm, ym, xp, yp)
    x2 = ring(after(xm, *one), "x", 1, "p2")
    y2 = ring(after(ym, *one), "y", 1, "p2")
    sib = swap(after(m, *one), "p2s")

    two = (x2, y2, sib, za)
    empty = jnp.zeros((1, 384, 384), FULL)
    a0 = jnp.concatenate([a[None], xm[None], xp[None], empty]).at[3].set(x2)
    b0 = jnp.concatenate([b[None], ym[None], yp[None], empty]).at[3].set(y2)
    a1, b1 = ring(after(a0, *two), "y", 1, "p3"), ring(after(b0, *two), "x", 1, "p3")
    a2, b2 = ring(after(a0, *two), "y", -1, "p3"), ring(after(b0, *two), "x", -1, "p3")
    zb = ring(after(jnp.concatenate([sib, za]), *two), "z", -1, "p3z")

    three = (a1, b1, a2, b2, zb)
    a3, b3 = ring(after(a1, *three), "y", 1, "p4"), ring(after(b1, *three), "x", 1, "p4")
    zt = swap(after(za, *three), "p4s")
    zs = swap(after(zb, *three), "p4s")

    pieces = dict(a0=a0, a1=a1, a2=a2, b0=b0, b1=b1, b2=b2, own=m, sib=sib, za=za, zb=zb)
    sums = products(0, where, mask, table, pieces, None, "early_products")
    pieces.update(zs=zs, zt=zt)
    sums = products(1, where, mask, table, pieces, sums, "middle_products")
    pieces.update(a3=a3, b3=b3)

    inverse = child_inverse[0]
    column = lax.broadcasted_iota(jnp.int32, (96, 768), 1)
    line = lax.broadcasted_iota(jnp.int32, (96, 768), 0) + row * 96
    diag_here = jnp.sum(jnp.where(column == line, inverse, 0.0), axis=0, keepdims=True)
    sep, part_var = last_products(where, mask, table, pieces, sums, coupling[0], diag_here)
    mine, other = pl.pallas_call(
        update_body,
        out_shape=(shape(4, 96, 768), shape(4, 96, 768)),
        in_specs=[SMEM, SMEM, VMEM, VMEM],
        out_specs=(VMEM, VMEM),
        compiler_params=pltpu.CompilerParams(vmem_limit_bytes=36 << 20),
        cost_estimate=cost(2),
        name="update",
    )(where, mask, coupling[0], sep)

    part = part_var + swap(part_var)
    half_sum = mine + swap(other)
    part = part + send(part, dz=1) + send(part, dz=-1) + send(part, dz=2)
    toward = lambda dz: lax.dynamic_index_in_dim(half_sum, (z + dz) % 4, 0, False)
    block_here = inverse + (toward(0) + send(toward(1), dz=1) + send(toward(-1), dz=-1) + send(toward(2), dz=2))
    part = after(part, half_sum)
    by_y = jnp.concatenate([part, send(part, dy=-1), send(part, dy=2), send(part, dy=1)], axis=0)
    by_xy = jnp.stack([by_y, send(by_y, dx=-1), send(by_y, dx=2), send(by_y, dx=1)])
    child = obs_node // 768
    far_x = (child // 4 - x) % 4
    far_y = (child % 4 - y) % 4
    index = (far_x * 4 + far_y) * 768 + obs_node % 768
    loo_var = by_xy.reshape(-1)[index] + obs_noise
    return sep[None], block_here[None], loo_var


def solution(mesh):
    placed = (
        P("row", "sub"),
        P("sub", "row", None),
        P("sub", "row", None),
        P("sub", None),
        P(("sub", "row")),
        P(("sub", "row")),
    )
    return jax.shard_map(
        local,
        mesh=mesh,
        in_specs=placed,
        out_specs=(P("sub", "row", None), P("sub", "row", None), P(("sub", "row"))),
        check_vma=False,
    )
```

```python
import jax
import jax.numpy as jnp
from jax import lax
from jax.experimental import pallas as pl
from jax.experimental.pallas import tpu as pltpu
from jax.sharding import PartitionSpec as P

AXES = ("sub", "row")
SHORT = jnp.bfloat16
FULL = jnp.float32


def place(x, y, z, c):
    return (x % 4) * 32 + (y % 4) * 8 + (z % 4) * 2 + c % 2


def send(value, dx=0, dy=0, dz=0, dc=0, turn=False):
    pairs = []
    for x in range(4):
        for y in range(4):
            for z in range(4):
                for c in range(2):
                    way = -1 if turn and c else 1
                    pairs.append((place(x, y, z, c), place(x + way * dx, y + way * dy, z + way * dz, c + dc)))
    return lax.ppermute(value, AXES, pairs)


def ring(value, axis, step, name):
    with jax.named_scope(name):
        return send(value, turn=True, **{"d" + axis: step})


def swap(value, name="swap"):
    with jax.named_scope(name):
        return send(value, dc=1)


def after(value, *earlier):
    return lax.optimization_barrier((value,) + earlier)[0]


def split(value):
    high = value.astype(SHORT)
    low = (value - high.astype(FULL)).astype(SHORT)
    return high, low


def dot3(a, b, dims):
    a_high, a_low = a
    b_high, b_low = b
    one = lambda u, v: lax.dot_general(u, v, (dims, ((), ())), preferred_element_type=FULL)
    return one(a_high, b_high) + (one(a_low, b_high) + one(a_high, b_low))


ROWS = ((1,), (0,))

LINES = ("a0", "a1", "a2", "a3", "b0", "b1", "b2", "b3")
BLOCKS = ("own", "sib", "za", "zb", "zc", "zu", "zs", "zt")


def work_table(x, y, z, core, way):
    unit = jnp.arange(32, dtype=jnp.int32)
    group, line, spot = unit // 16, unit // 4 % 4, unit % 4
    step = lambda k: jnp.where(k == 3, 2, jnp.where(k == 0, 0, 2 * k - 3))
    x_step = jnp.where(group == 0, step(spot), step(line))
    y_step = jnp.where(group == 0, step(line), step(spot))
    at_x = (x + way * x_step) & 3
    at_y = (y + way * y_step) & 3
    far = ((at_x - z) * way) & 3
    half = (far * 2 + ((at_y >> 1) ^ core)) * 2 + (at_y & 1)
    rank = jnp.where(line == 3, 2, jnp.where((line == 2) | (far == 2), 1, 0))
    early = jnp.sum((rank.reshape(2, 16) == 0).astype(jnp.int32), axis=1)
    key = (group * 3 + rank) * 32 + unit
    order = jnp.sum((key[None, :] < key[:, None]).astype(jnp.int32), axis=1)
    here = (order[None, :] == unit[:, None]).astype(jnp.int32)
    pick = lambda v: jnp.sum(here * v[None, :], axis=1)
    return jnp.stack([pick(unit), pick(half), pick(at_x * 4 + at_y)]), early


def pair_loop(begin, end, refs, table, mask, sums, meanwhile, s_buf, m_buf, spot, s_sem, m_sem):
    first_group = end[0] - begin[0]
    count = first_group + end[1] - begin[1]

    def start(q, slot):
        group = jnp.where(q < first_group, 0, 1)
        pair = jnp.where(q < first_group, begin[0] + q, begin[1] + q - first_group)
        spot[slot, 2] = group
        for part in range(2):
            entry = group * 16 + pair * 2 + part
            unit = table[0, entry]
            half = table[1, entry]
            spot[slot, part] = table[2, entry]
            s_target = s_buf.at[slot, :, pl.ds(part * 384, 384)]
            m_target = m_buf.at[slot, pl.ds(part * 384, 384), :]
            for number, name in enumerate(LINES):
                if name in refs:

                    @pl.when(unit >> 2 == number)
                    def _():
                        pltpu.make_async_copy(refs[name].at[unit & 3], s_target, s_sem.at[slot, part]).start()

            for number, name in enumerate(BLOCKS):
                if name in refs:

                    @pl.when(half >> 1 == number)
                    def _():
                        pltpu.make_async_copy(refs[name].at[half & 1], m_target, m_sem.at[slot, part]).start()

    def finish(slot):
        for part in range(2):
            target = s_buf.at[slot, :, pl.ds(part * 384, 384)]
            pltpu.make_async_copy(refs["a0"].at[0], target, s_sem.at[slot, part]).wait()
            target = m_buf.at[slot, pl.ds(part * 384, 384), :]
            pltpu.make_async_copy(refs["own"].at[0], target, m_sem.at[slot, part]).wait()
        pieces = []
        for part in range(2):
            block = spot[slot, part]
            for third in range(3):
                factor = mask[(block * 3 + third) >> 1].astype(FULL)
                pieces.append(m_buf[slot, pl.ds(part * 384 + third * 128, 128), :] * factor)
        part_sum = dot3(split(s_buf[slot]), split(jnp.concatenate(pieces, axis=0)), ROWS)
        group = spot[slot, 2]
        sums[group] = sums[group] + part_sum

    start(0, 0)
    if meanwhile is not None:
        meanwhile()

    def step(p, carry):
        @pl.when(p + 1 < count)
        def _():
            start(p + 1, (p + 1) % 2)

        finish(p % 2)
        return carry

    lax.fori_loop(0, count, step, 0)


HBM = pl.BlockSpec(memory_space=pl.ANY)
SMEM = pl.BlockSpec(memory_space=pltpu.SMEM)
VMEM = pl.BlockSpec(memory_space=pltpu.VMEM)


def buffers():
    return [
        pltpu.VMEM((2, 384, 768), FULL),
        pltpu.VMEM((2, 768, 768), FULL),
        pltpu.SMEM((2, 3), jnp.int32),
        pltpu.SemaphoreType.DMA((2, 2)),
        pltpu.SemaphoreType.DMA((2, 2)),
    ]


def shape(*dims):
    return jax.ShapeDtypeStruct(dims, FULL)


def cost(pairs):
    return pl.CostEstimate(flops=1_400_000_000 * pairs, bytes_accessed=3_600_000 * pairs, transcendentals=0)


def early_products(where, mask, table, pieces):
    names = list(pieces)

    def body(where_ref, mask_ref, table_ref, *rest):
        refs = dict(zip(names, rest))
        sums, *scratch = rest[len(names) :]

        def meanwhile():
            sums[...] = jnp.zeros_like(sums)

        end = (where_ref[6] // 2, where_ref[7] // 2)
        pair_loop((0, 0), end, refs, table_ref, mask_ref, sums, meanwhile, *scratch)

    return pl.pallas_call(
        body,
        out_shape=shape(2, 384, 768),
        in_specs=[SMEM, SMEM, SMEM] + [HBM] * len(names),
        out_specs=VMEM,
        scratch_shapes=buffers(),
        compiler_params=pltpu.CompilerParams(vmem_limit_bytes=60 << 20),
        cost_estimate=cost(6),
        name="early_products",
    )(where, mask, table, *pieces.values())


def middle_products(where, mask, table, pieces, before):
    names = list(pieces)

    def body(where_ref, mask_ref, table_ref, *rest):
        refs = dict(zip(names, rest))
        before_ref, own_ref, sums, own_high, own_low, sem, *scratch = rest[len(names) :]
        copy = pltpu.make_async_copy(before_ref, sums, sem)
        copy.start()

        def meanwhile():
            row = where_ref[5]
            tiles = [
                mask_ref[row * 3 + k].astype(FULL) * own_ref[pl.ds(k * 256, 256), :] for k in range(3)
            ]
            high, low = split(jnp.concatenate(tiles, axis=0).T)
            own_high[...] = high
            own_low[...] = low
            copy.wait()

        early = (where_ref[6] // 2, where_ref[7] // 2)
        pair_loop(early, (6, 6), refs, table_ref, mask_ref, sums, meanwhile, *scratch)

    half = jax.ShapeDtypeStruct((768, 768), SHORT)
    return pl.pallas_call(
        body,
        out_shape=(shape(2, 384, 768), half, half),
        in_specs=[SMEM, SMEM, SMEM] + [HBM] * (len(names) + 1) + [VMEM],
        out_specs=(VMEM, VMEM, VMEM),
        scratch_shapes=[pltpu.SemaphoreType.DMA] + buffers(),
        compiler_params=pltpu.CompilerParams(vmem_limit_bytes=60 << 20),
        cost_estimate=cost(6),
        name="middle_products",
    )(where, mask, table, *pieces.values(), before, pieces["own"].reshape(768, 768))


def last_products(where, mask, table, pieces, before, own_high, own_low, diag_here):
    names = list(pieces)

    def body(where_ref, mask_ref, table_ref, *rest):
        refs = dict(zip(names, rest))
        before_ref, high_ref, low_ref, diag_ref, sep, part_var, mine, other = rest[len(names) : len(names) + 8]
        sums, minus, high, low, sems, *scratch = rest[len(names) + 8 :]
        core = where_ref[3]
        copies = [
            pltpu.make_async_copy(before_ref, sums, sems.at[0]),
            pltpu.make_async_copy(high_ref, high, sems.at[1]),
            pltpu.make_async_copy(low_ref, low, sems.at[2]),
        ]

        def meanwhile():
            for copy in copies:
                copy.start()
            copies[0].wait()

        pair_loop((6, 6), (8, 8), refs, table_ref, mask_ref, sums, meanwhile, *scratch)
        product = jnp.concatenate([sums[0], sums[1]], axis=0)
        minus[...] = -product
        put = pltpu.make_async_copy(minus, sep, sems.at[3])
        put.start()
        copies[1].wait()
        copies[2].wait()
        update = dot3((high[...], low[...]), split(product), ROWS)
        row = lax.broadcasted_iota(jnp.int32, (768, 768), 0)
        column = lax.broadcasted_iota(jnp.int32, (768, 768), 1)
        part_var[...] = diag_ref[...] + jnp.sum(jnp.where(row == column, update, 0.0), axis=0, keepdims=True)
        for zz in range(4):
            lower = update[zz * 192 : zz * 192 + 96]
            upper = update[zz * 192 + 96 : zz * 192 + 192]

            @pl.when(core == 0)
            def _():
                mine[zz] = lower
                other[zz] = upper

            @pl.when(core != 0)
            def _():
                mine[zz] = upper
                other[zz] = lower

        put.wait()

    return pl.pallas_call(
        body,
        out_shape=(shape(768, 768), shape(1, 768), shape(4, 96, 768), shape(4, 96, 768)),
        in_specs=[SMEM, SMEM, SMEM] + [HBM] * (len(names) + 3) + [VMEM],
        out_specs=(HBM, VMEM, VMEM, VMEM),
        scratch_shapes=[
            pltpu.VMEM((2, 384, 768), FULL),
            pltpu.VMEM((768, 768), FULL),
            pltpu.VMEM((768, 768), SHORT),
            pltpu.VMEM((768, 768), SHORT),
            pltpu.SemaphoreType.DMA((4,)),
        ]
        + buffers(),
        compiler_params=pltpu.CompilerParams(vmem_limit_bytes=60 << 20),
        cost_estimate=cost(6),
        name="last_products",
    )(where, mask, table, *pieces.values(), before, own_high, own_low, diag_here)


def local(sigma_top, coupling, child_inverse, tile_mask, obs_node, obs_noise):
    sub = lax.axis_index("sub")
    row = lax.axis_index("row")
    x, y, z, core = sub // 4, sub % 4, row // 2, row % 2
    way = 1 - 2 * core
    table, early = work_table(x, y, z, core, way)
    where = jnp.concatenate([jnp.stack([x, y, z, core, way, row]).astype(jnp.int32), early])
    mask = tile_mask[0]

    inverse = child_inverse[0]
    column = lax.broadcasted_iota(jnp.int32, (96, 768), 1)
    line = lax.broadcasted_iota(jnp.int32, (96, 768), 0) + row * 96
    diag_here = jnp.sum(jnp.where(column == line, inverse, 0.0), axis=0, keepdims=True)
    child = obs_node // 768
    far_x = (child // 4 - x) % 4
    far_y = (child % 4 - y) % 4
    index = (far_x * 4 + far_y) * 768 + obs_node % 768

    a = sigma_top[:384]
    b = sigma_top[384:]
    m = coupling[0].reshape(2, 384, 768)
    za = ring(m, "z", -1, "p1z")
    xm, ym = ring(a, "x", 1, "p1"), ring(b, "y", 1, "p1")
    xp, yp = ring(a, "x", -1, "p1"), ring(b, "y", -1, "p1")

    one = (xm, ym, xp, yp)
    x2, y2 = ring(after(xm, *one), "x", 1, "p2"), ring(after(ym, *one), "y", 1, "p2")
    sib = swap(after(m, *one), "p2s")

    two = (x2, y2, sib, za)
    empty = jnp.zeros((1, 384, 384), FULL)
    a0 = jnp.concatenate([a[None], xm[None], xp[None], empty]).at[3].set(x2)
    b0 = jnp.concatenate([b[None], ym[None], yp[None], empty]).at[3].set(y2)
    a1, b1 = ring(after(a0, *two), "y", 1, "p3"), ring(after(b0, *two), "x", 1, "p3")
    zb = ring(after(sib, *two), "z", -1, "p3z")

    three = (a1, b1, zb, table, where, diag_here, index)
    a2, b2 = ring(after(a0, *three), "y", -1, "p4"), ring(after(b0, *three), "x", -1, "p4")
    zc = ring(after(za, *three), "z", -1, "p4z")
    zs = swap(after(zb, *three), "p4s")
    zt = swap(after(za, *three), "p4s")
    pieces = dict(a0=a0, a1=a1, b0=b0, b1=b1, own=m, sib=sib, za=za, zb=zb, zs=zs, zt=zt)
    sums = early_products(where, mask, table, pieces)

    four = (a2, b2, zc, zs, zt, sums)
    a3, b3 = ring(after(a1, *four), "y", 1, "p5"), ring(after(b1, *four), "x", 1, "p5")
    zu = swap(after(zc, *four), "p5s")
    pieces.update(a2=a2, b2=b2, zc=zc, zu=zu)
    sums, own_high, own_low = middle_products(where, mask, table, pieces, sums)

    pieces.update(a3=a3, b3=b3)
    sep, part_var, mine, other = last_products(where, mask, table, pieces, sums, own_high, own_low, diag_here)

    part = part_var + swap(part_var)
    half_sum = mine + swap(other)
    part = part + send(part, dz=1) + send(part, dz=-1) + send(part, dz=2)
    toward = lambda dz: lax.dynamic_index_in_dim(half_sum, (z + dz) % 4, 0, False)
    block_here = inverse + (toward(0) + send(toward(1), dz=1) + send(toward(-1), dz=-1) + send(toward(2), dz=2))
    part = after(part, half_sum)
    by_y = jnp.concatenate([part, send(part, dy=-1), send(part, dy=2), send(part, dy=1)], axis=0)
    by_xy = jnp.stack([by_y, send(by_y, dx=-1), send(by_y, dx=2), send(by_y, dx=1)])
    loo_var = by_xy.reshape(-1)[index] + obs_noise
    return sep[None], block_here[None], loo_var


def solution(mesh):
    placed = (
        P("row", "sub"),
        P("sub", "row", None),
        P("sub", "row", None),
        P("sub", None),
        P(("sub", "row")),
        P(("sub", "row")),
    )
    return jax.shard_map(
        local,
        mesh=mesh,
        in_specs=placed,
        out_specs=(P("sub", "row", None), P("sub", "row", None), P(("sub", "row"))),
        check_vma=False,
    )
```

```python
import jax
import jax.numpy as jnp
from jax import lax
from jax.experimental import pallas as pl
from jax.experimental.pallas import tpu as pltpu
from jax.sharding import PartitionSpec as P

AXES = ("sub", "row")
SHORT = jnp.bfloat16
FULL = jnp.float32


def place(x, y, z, c):
    return (x % 4) * 32 + (y % 4) * 8 + (z % 4) * 2 + c % 2


def send(value, dx=0, dy=0, dz=0, dc=0, turn=False):
    pairs = []
    for x in range(4):
        for y in range(4):
            for z in range(4):
                for c in range(2):
                    way = -1 if turn and c else 1
                    pairs.append((place(x, y, z, c), place(x + way * dx, y + way * dy, z + way * dz, c + dc)))
    return lax.ppermute(value, AXES, pairs)


def ring(value, axis, step, name):
    with jax.named_scope(name):
        return send(value, turn=True, **{"d" + axis: step})


def swap(value, name="swap"):
    with jax.named_scope(name):
        return send(value, dc=1)


def after(value, *earlier):
    return lax.optimization_barrier((value,) + earlier)[0]


def split(value):
    high = value.astype(SHORT)
    low = (value - high.astype(FULL)).astype(SHORT)
    return high, low


def dot3(a, b, dims):
    a_high, a_low = a
    b_high, b_low = b
    one = lambda u, v: lax.dot_general(u, v, (dims, ((), ())), preferred_element_type=FULL)
    return one(a_high, b_high) + (one(a_low, b_high) + one(a_high, b_low))


ROWS = ((1,), (0,))
SLOTS = 3

LINES = ("a0", "a1", "a2", "a3", "b0", "b1", "b2", "b3")
BLOCKS = ("own", "sib", "za", "zb", "zc", "zu", "zs", "zt")


def work_table(x, y, z, core, way):
    unit = jnp.arange(32, dtype=jnp.int32)
    group, line, spot = unit // 16, unit // 4 % 4, unit % 4
    step = lambda k: jnp.where(k == 3, 2, jnp.where(k == 0, 0, 2 * k - 3))
    x_step = jnp.where(group == 0, step(spot), step(line))
    y_step = jnp.where(group == 0, step(line), step(spot))
    at_x = (x + way * x_step) & 3
    at_y = (y + way * y_step) & 3
    far = ((z - at_x) * way) & 3
    half = (far * 2 + ((at_y >> 1) ^ core)) * 2 + (at_y & 1)
    rank = jnp.where(line == 3, 2, jnp.where((line == 2) | (far == 2), 1, 0))
    early = jnp.sum((rank.reshape(2, 16) == 0).astype(jnp.int32), axis=1)
    key = (group * 3 + rank) * 32 + unit
    order = jnp.sum((key[None, :] < key[:, None]).astype(jnp.int32), axis=1)
    here = (order[None, :] == unit[:, None]).astype(jnp.int32)
    pick = lambda v: jnp.sum(here * v[None, :], axis=1)
    return jnp.stack([pick(unit), pick(half), pick(at_x * 4 + at_y)]), early


def pair_loop(begin, end, refs, table, mask, sums, meanwhile, s_buf, m_buf, spot, s_sem, m_sem):
    first_group = end[0] - begin[0]
    count = first_group + end[1] - begin[1]

    def start(q, slot):
        group = jnp.where(q < first_group, 0, 1)
        pair = jnp.where(q < first_group, begin[0] + q, begin[1] + q - first_group)
        spot[slot, 2] = group
        for part in range(2):
            entry = group * 16 + pair * 2 + part
            unit = table[0, entry]
            half = table[1, entry]
            spot[slot, part] = table[2, entry]
            s_target = s_buf.at[slot, :, pl.ds(part * 384, 384)]
            m_target = m_buf.at[slot, pl.ds(part * 384, 384), :]
            for number, name in enumerate(LINES):
                if name in refs:

                    @pl.when(unit >> 2 == number)
                    def _():
                        pltpu.make_async_copy(refs[name].at[unit & 3], s_target, s_sem.at[slot, part]).start()

            for number, name in enumerate(BLOCKS):
                if name in refs:

                    @pl.when(half >> 1 == number)
                    def _():
                        pltpu.make_async_copy(refs[name].at[half & 1], m_target, m_sem.at[slot, part]).start()

    def finish(slot):
        for part in range(2):
            target = s_buf.at[slot, :, pl.ds(part * 384, 384)]
            pltpu.make_async_copy(refs["b0" if "b0" in refs else "b3"].at[0], target, s_sem.at[slot, part]).wait()
            target = m_buf.at[slot, pl.ds(part * 384, 384), :]
            pltpu.make_async_copy(refs["own"].at[0], target, m_sem.at[slot, part]).wait()
        pieces = []
        for part in range(2):
            block = spot[slot, part]
            for third in range(3):
                factor = mask[(block * 3 + third) >> 1].astype(FULL)
                pieces.append(m_buf[slot, pl.ds(part * 384 + third * 128, 128), :] * factor)
        part_sum = dot3(split(s_buf[slot]), split(jnp.concatenate(pieces, axis=0)), ROWS)
        group = spot[slot, 2]
        sums[group] = sums[group] + part_sum

    for ahead in range(SLOTS - 1):

        @pl.when(ahead < count)
        def _():
            start(ahead, ahead)

    if meanwhile is not None:
        meanwhile()

    def step(p, carry):
        later = p + SLOTS - 1

        @pl.when(later < count)
        def _():
            start(later, lax.rem(later, SLOTS))

        finish(lax.rem(p, SLOTS))
        return carry

    lax.fori_loop(0, count, step, 0)


HBM = pl.BlockSpec(memory_space=pl.ANY)
SMEM = pl.BlockSpec(memory_space=pltpu.SMEM)
VMEM = pl.BlockSpec(memory_space=pltpu.VMEM)


def buffers():
    return [
        pltpu.VMEM((SLOTS, 384, 768), FULL),
        pltpu.VMEM((SLOTS, 768, 768), FULL),
        pltpu.SMEM((SLOTS, 3), jnp.int32),
        pltpu.SemaphoreType.DMA((SLOTS, 2)),
        pltpu.SemaphoreType.DMA((SLOTS, 2)),
    ]


def shape(*dims):
    return jax.ShapeDtypeStruct(dims, FULL)


def cost(pairs):
    return pl.CostEstimate(flops=1_400_000_000 * pairs, bytes_accessed=3_600_000 * pairs, transcendentals=0)


def early_products(where, mask, table, pieces):
    names = list(pieces)

    def body(where_ref, mask_ref, table_ref, *rest):
        refs = dict(zip(names, rest))
        sums, *scratch = rest[len(names) :]

        def meanwhile():
            sums[...] = jnp.zeros_like(sums)

        end = (where_ref[6] // 2, where_ref[7] // 2)
        pair_loop((0, 0), end, refs, table_ref, mask_ref, sums, meanwhile, *scratch)

    return pl.pallas_call(
        body,
        out_shape=shape(2, 384, 768),
        in_specs=[SMEM, SMEM, SMEM] + [HBM] * len(names),
        out_specs=VMEM,
        scratch_shapes=buffers(),
        compiler_params=pltpu.CompilerParams(vmem_limit_bytes=60 << 20),
        cost_estimate=cost(6),
        name="early_products",
    )(where, mask, table, *pieces.values())


def middle_products(where, mask, table, pieces, before):
    names = list(pieces)

    def body(where_ref, mask_ref, table_ref, *rest):
        refs = dict(zip(names, rest))
        before_ref, own_ref, sums, own_high, own_low, sem, *scratch = rest[len(names) :]
        copy = pltpu.make_async_copy(before_ref, sums, sem)
        copy.start()

        def meanwhile():
            row = where_ref[5]
            tiles = [
                mask_ref[row * 3 + k].astype(FULL) * own_ref[pl.ds(k * 256, 256), :] for k in range(3)
            ]
            high, low = split(jnp.concatenate(tiles, axis=0).T)
            own_high[...] = high
            own_low[...] = low
            copy.wait()

        early = (where_ref[6] // 2, where_ref[7] // 2)
        pair_loop(early, (6, 6), refs, table_ref, mask_ref, sums, meanwhile, *scratch)

    half = jax.ShapeDtypeStruct((768, 768), SHORT)
    return pl.pallas_call(
        body,
        out_shape=(shape(2, 384, 768), half, half),
        in_specs=[SMEM, SMEM, SMEM] + [HBM] * (len(names) + 1) + [VMEM],
        out_specs=(VMEM, VMEM, VMEM),
        scratch_shapes=[pltpu.SemaphoreType.DMA] + buffers(),
        compiler_params=pltpu.CompilerParams(vmem_limit_bytes=60 << 20),
        cost_estimate=cost(6),
        name="middle_products",
    )(where, mask, table, *pieces.values(), before, pieces["own"].reshape(768, 768))


def last_products(where, mask, table, pieces, before, own_high, own_low, diag_here):
    names = list(pieces)

    def body(where_ref, mask_ref, table_ref, *rest):
        refs = dict(zip(names, rest))
        before_ref, high_ref, low_ref, diag_ref, sep, part_var, mine, other = rest[len(names) : len(names) + 8]
        sums, minus, high, low, sems, *scratch = rest[len(names) + 8 :]
        core = where_ref[3]
        copies = [
            pltpu.make_async_copy(before_ref, sums, sems.at[0]),
            pltpu.make_async_copy(high_ref, high, sems.at[1]),
            pltpu.make_async_copy(low_ref, low, sems.at[2]),
        ]

        def meanwhile():
            for copy in copies:
                copy.start()
            copies[0].wait()

        pair_loop((6, 6), (8, 8), refs, table_ref, mask_ref, sums, meanwhile, *scratch)
        product = jnp.concatenate([sums[0], sums[1]], axis=0)
        minus[...] = -product
        put = pltpu.make_async_copy(minus, sep, sems.at[3])
        put.start()
        copies[1].wait()
        copies[2].wait()
        update = dot3((high[...], low[...]), split(product), ROWS)
        row = lax.broadcasted_iota(jnp.int32, (768, 768), 0)
        column = lax.broadcasted_iota(jnp.int32, (768, 768), 1)
        part_var[...] = diag_ref[...] + jnp.sum(jnp.where(row == column, update, 0.0), axis=0, keepdims=True)
        for zz in range(4):
            lower = update[zz * 192 : zz * 192 + 96]
            upper = update[zz * 192 + 96 : zz * 192 + 192]

            @pl.when(core == 0)
            def _():
                mine[zz] = lower
                other[zz] = upper

            @pl.when(core != 0)
            def _():
                mine[zz] = upper
                other[zz] = lower

        put.wait()

    return pl.pallas_call(
        body,
        out_shape=(shape(768, 768), shape(1, 768), shape(4, 96, 768), shape(4, 96, 768)),
        in_specs=[SMEM, SMEM, SMEM] + [HBM] * (len(names) + 3) + [VMEM],
        out_specs=(HBM, VMEM, VMEM, VMEM),
        scratch_shapes=[
            pltpu.VMEM((2, 384, 768), FULL),
            pltpu.VMEM((768, 768), FULL),
            pltpu.VMEM((768, 768), SHORT),
            pltpu.VMEM((768, 768), SHORT),
            pltpu.SemaphoreType.DMA((4,)),
        ]
        + buffers(),
        compiler_params=pltpu.CompilerParams(vmem_limit_bytes=60 << 20),
        cost_estimate=cost(6),
        name="last_products",
    )(where, mask, table, *pieces.values(), before, own_high, own_low, diag_here)


def local(sigma_top, coupling, child_inverse, tile_mask, obs_node, obs_noise):
    sub = lax.axis_index("sub")
    row = lax.axis_index("row")
    x, y, z, core = sub // 4, sub % 4, row // 2, row % 2
    way = 1 - 2 * core
    table, early = work_table(x, y, z, core, way)
    where = jnp.concatenate([jnp.stack([x, y, z, core, way, row]).astype(jnp.int32), early])
    mask = tile_mask[0]

    inverse = child_inverse[0]
    column = lax.broadcasted_iota(jnp.int32, (96, 768), 1)
    line = lax.broadcasted_iota(jnp.int32, (96, 768), 0) + row * 96
    diag_here = jnp.sum(jnp.where(column == line, inverse, 0.0), axis=0, keepdims=True)
    child = obs_node // 768
    far_x = (child // 4 - x) % 4
    far_y = (child % 4 - y) % 4
    index = (far_x * 4 + far_y) * 768 + obs_node % 768

    a = sigma_top[:384]
    b = sigma_top[384:]
    m = coupling[0].reshape(2, 384, 768)
    za = ring(m, "z", 1, "p1z")
    xm, ym = ring(a, "x", 1, "p1"), ring(b, "y", 1, "p1")
    xp, yp = ring(a, "x", -1, "p1"), ring(b, "y", -1, "p1")

    one = (xm, ym, xp, yp)
    x2, y2 = ring(after(xm, *one), "x", 1, "p2"), ring(after(ym, *one), "y", 1, "p2")
    sib = swap(after(m, *one), "p2s")

    two = (x2, y2, sib, za)
    empty = jnp.zeros((1, 384, 384), FULL)
    a0 = jnp.concatenate([a[None], xm[None], xp[None], empty]).at[3].set(x2)
    b0 = jnp.concatenate([b[None], ym[None], yp[None], empty]).at[3].set(y2)
    a1, b1 = ring(after(a0, *two), "y", 1, "p3"), ring(after(b0, *two), "x", 1, "p3")
    zb = ring(after(sib, *two), "z", 1, "p3z")

    three = (a1, b1, zb, table, where, diag_here, index)
    a2, b2 = ring(after(a0, *three), "y", -1, "p4"), ring(after(b0, *three), "x", -1, "p4")
    zc = ring(after(za, *three), "z", 1, "p4z")
    zs = swap(after(zb, *three), "p4s")
    zt = swap(after(za, *three), "p4s")
    pieces = dict(a0=a0, a1=a1, b0=b0, b1=b1, own=m, sib=sib, za=za, zb=zb, zs=zs, zt=zt)
    sums = early_products(where, mask, table, pieces)

    four = (a2, b2, zc, zs, zt, sums)
    a3, b3 = ring(after(a1, *four), "y", 1, "p5"), ring(after(b1, *four), "x", 1, "p5")
    zu = swap(after(zc, *four), "p5s")
    pieces.update(a2=a2, b2=b2, zc=zc, zu=zu)
    sums, own_high, own_low = middle_products(where, mask, table, pieces, sums)

    pieces.update(a3=a3, b3=b3)
    final = {name: pieces[name] for name in BLOCKS + ("a3", "b3")}
    sep, part_var, mine, other = last_products(where, mask, table, final, sums, own_high, own_low, diag_here)

    part = part_var + swap(part_var)
    half_sum = mine + swap(other)
    part = part + send(part, dz=1) + send(part, dz=-1) + send(part, dz=2)
    toward = lambda dz: lax.dynamic_index_in_dim(half_sum, (z + dz) % 4, 0, False)
    block_here = inverse + (toward(0) + send(toward(1), dz=1) + send(toward(-1), dz=-1) + send(toward(2), dz=2))
    part = after(part, half_sum)
    by_y = jnp.concatenate([part, send(part, dy=-1), send(part, dy=2), send(part, dy=1)], axis=0)
    by_xy = jnp.stack([by_y, send(by_y, dx=-1), send(by_y, dx=2), send(by_y, dx=1)])
    loo_var = by_xy.reshape(-1)[index] + obs_noise
    return sep[None], block_here[None], loo_var


def solution(mesh):
    placed = (
        P("row", "sub"),
        P("sub", "row", None),
        P("sub", "row", None),
        P("sub", None),
        P(("sub", "row")),
        P(("sub", "row")),
    )
    return jax.shard_map(
        local,
        mesh=mesh,
        in_specs=placed,
        out_specs=(P("sub", "row", None), P("sub", "row", None), P(("sub", "row"))),
        check_vma=False,
    )
```

```python
import jax
import jax.numpy as jnp
from jax import lax
from jax.experimental import pallas as pl
from jax.experimental.pallas import tpu as pltpu
from jax.sharding import PartitionSpec as P

AXES = ("sub", "row")
SHORT = jnp.bfloat16
FULL = jnp.float32


def place(x, y, z, c):
    return (x % 4) * 32 + (y % 4) * 8 + (z % 4) * 2 + c % 2


def send(value, dx=0, dy=0, dz=0, dc=0, turn=False):
    pairs = []
    for x in range(4):
        for y in range(4):
            for z in range(4):
                for c in range(2):
                    way = -1 if turn and c else 1
                    pairs.append((place(x, y, z, c), place(x + way * dx, y + way * dy, z + way * dz, c + dc)))
    return lax.ppermute(value, AXES, pairs)


def ring(value, axis, step, name):
    with jax.named_scope(name):
        return send(value, turn=True, **{"d" + axis: step})


def swap(value, name="swap"):
    with jax.named_scope(name):
        return send(value, dc=1)


def after(value, *earlier):
    return lax.optimization_barrier((value,) + earlier)[0]


def split(value):
    high = value.astype(SHORT)
    low = (value - high.astype(FULL)).astype(SHORT)
    return high, low


def dot3(a, b, dims):
    a_high, a_low = a
    b_high, b_low = b
    one = lambda u, v: lax.dot_general(u, v, (dims, ((), ())), preferred_element_type=FULL)
    return one(a_high, b_high) + (one(a_low, b_high) + one(a_high, b_low))


ROWS = ((1,), (0,))
SLOTS = 3

LINES = ("a0", "a1", "a2", "a3", "b0", "b1", "b2", "b3")
BLOCKS = ("own", "sib", "za", "zb", "zc", "zu", "zs", "zt")


def work_table(x, y, z, core, way):
    unit = jnp.arange(32, dtype=jnp.int32)
    group, line, spot = unit // 16, unit // 4 % 4, unit % 4
    step = lambda k: jnp.where(k == 3, 2, jnp.where(k == 0, 0, 2 * k - 3))
    x_step = jnp.where(group == 0, step(spot), step(line))
    y_step = jnp.where(group == 0, step(line), step(spot))
    at_x = (x + way * x_step) & 3
    at_y = (y + way * y_step) & 3
    far = ((z - at_x) * way) & 3
    half = (far * 2 + ((at_y >> 1) ^ core)) * 2 + (at_y & 1)
    rank = jnp.where(line == 3, 2, jnp.where((line == 2) | (far == 2), 1, 0))
    early = jnp.sum((rank.reshape(2, 16) == 0).astype(jnp.int32), axis=1)
    key = (group * 3 + rank) * 32 + unit
    order = jnp.sum((key[None, :] < key[:, None]).astype(jnp.int32), axis=1)
    here = (order[None, :] == unit[:, None]).astype(jnp.int32)
    pick = lambda v: jnp.sum(here * v[None, :], axis=1)
    return jnp.stack([pick(unit), pick(half), pick(at_x * 4 + at_y)]), early


def pair_loop(begin, end, refs, table, mask, sums, meanwhile, s_buf, m_buf, spot, s_sem, m_sem):
    first_group = end[0] - begin[0]
    count = first_group + end[1] - begin[1]

    def start(q, slot):
        group = jnp.where(q < first_group, 0, 1)
        pair = jnp.where(q < first_group, begin[0] + q, begin[1] + q - first_group)
        spot[slot, 2] = group
        for part in range(2):
            entry = group * 16 + pair * 2 + part
            unit = table[0, entry]
            half = table[1, entry]
            spot[slot, part] = table[2, entry]
            s_target = s_buf.at[slot, :, pl.ds(part * 384, 384)]
            m_target = m_buf.at[slot, pl.ds(part * 384, 384), :]
            for number, name in enumerate(LINES):
                if name in refs:

                    @pl.when(unit >> 2 == number)
                    def _():
                        pltpu.make_async_copy(refs[name].at[unit & 3], s_target, s_sem.at[slot, part]).start()

            for number, name in enumerate(BLOCKS):
                if name in refs:

                    @pl.when(half >> 1 == number)
                    def _():
                        pltpu.make_async_copy(refs[name].at[half & 1], m_target, m_sem.at[slot, part]).start()

    def finish(slot):
        for part in range(2):
            target = s_buf.at[slot, :, pl.ds(part * 384, 384)]
            pltpu.make_async_copy(refs["b0" if "b0" in refs else "b3"].at[0], target, s_sem.at[slot, part]).wait()
            target = m_buf.at[slot, pl.ds(part * 384, 384), :]
            pltpu.make_async_copy(refs["own"].at[0], target, m_sem.at[slot, part]).wait()
        pieces = []
        for part in range(2):
            block = spot[slot, part]
            for third in range(3):
                factor = mask[(block * 3 + third) >> 1].astype(FULL)
                pieces.append(m_buf[slot, pl.ds(part * 384 + third * 128, 128), :] * factor)
        part_sum = dot3(split(s_buf[slot]), split(jnp.concatenate(pieces, axis=0)), ROWS)
        group = spot[slot, 2]
        sums[group] = sums[group] + part_sum

    for ahead in range(SLOTS - 1):

        @pl.when(ahead < count)
        def _():
            start(ahead, ahead)

    if meanwhile is not None:
        meanwhile()

    def step(p, carry):
        later = p + SLOTS - 1

        @pl.when(later < count)
        def _():
            start(later, lax.rem(later, SLOTS))

        finish(lax.rem(p, SLOTS))
        return carry

    lax.fori_loop(0, count, step, 0)


HBM = pl.BlockSpec(memory_space=pl.ANY)
SMEM = pl.BlockSpec(memory_space=pltpu.SMEM)
VMEM = pl.BlockSpec(memory_space=pltpu.VMEM)


def buffers():
    return [
        pltpu.VMEM((SLOTS, 384, 768), FULL),
        pltpu.VMEM((SLOTS, 768, 768), FULL),
        pltpu.SMEM((SLOTS, 3), jnp.int32),
        pltpu.SemaphoreType.DMA((SLOTS, 2)),
        pltpu.SemaphoreType.DMA((SLOTS, 2)),
    ]


def shape(*dims):
    return jax.ShapeDtypeStruct(dims, FULL)


def cost(pairs):
    return pl.CostEstimate(flops=1_400_000_000 * pairs, bytes_accessed=3_600_000 * pairs, transcendentals=0)


def early_products(where, mask, table, pieces):
    names = list(pieces)

    def body(where_ref, mask_ref, table_ref, *rest):
        refs = dict(zip(names, rest))
        sums, *scratch = rest[len(names) :]

        def meanwhile():
            sums[...] = jnp.zeros_like(sums)

        end = (where_ref[6] // 2, where_ref[7] // 2)
        pair_loop((0, 0), end, refs, table_ref, mask_ref, sums, meanwhile, *scratch)

    return pl.pallas_call(
        body,
        out_shape=shape(2, 384, 768),
        in_specs=[SMEM, SMEM, SMEM] + [HBM] * len(names),
        out_specs=VMEM,
        scratch_shapes=buffers(),
        compiler_params=pltpu.CompilerParams(vmem_limit_bytes=60 << 20),
        cost_estimate=cost(6),
        name="early_products",
    )(where, mask, table, *pieces.values())


def middle_products(where, mask, table, pieces, before):
    names = list(pieces)

    def body(where_ref, mask_ref, table_ref, *rest):
        refs = dict(zip(names, rest))
        before_ref, own_ref, sums, own_high, own_low, sem, *scratch = rest[len(names) :]
        copy = pltpu.make_async_copy(before_ref, sums, sem)
        copy.start()

        def meanwhile():
            row = where_ref[5]
            tiles = [
                mask_ref[row * 3 + k].astype(FULL) * own_ref[pl.ds(k * 256, 256), :] for k in range(3)
            ]
            high, low = split(jnp.concatenate(tiles, axis=0).T)
            own_high[...] = high
            own_low[...] = low
            copy.wait()

        early = (where_ref[6] // 2, where_ref[7] // 2)
        pair_loop(early, (6, 6), refs, table_ref, mask_ref, sums, meanwhile, *scratch)

    half = jax.ShapeDtypeStruct((768, 768), SHORT)
    return pl.pallas_call(
        body,
        out_shape=(shape(2, 384, 768), half, half),
        in_specs=[SMEM, SMEM, SMEM] + [HBM] * (len(names) + 1) + [VMEM],
        out_specs=(VMEM, VMEM, VMEM),
        scratch_shapes=[pltpu.SemaphoreType.DMA] + buffers(),
        compiler_params=pltpu.CompilerParams(vmem_limit_bytes=60 << 20),
        cost_estimate=cost(6),
        name="middle_products",
    )(where, mask, table, *pieces.values(), before, pieces["own"].reshape(768, 768))


def last_products(where, mask, table, pieces, before, own_high, own_low, diag_here):
    names = list(pieces)

    def body(where_ref, mask_ref, table_ref, *rest):
        refs = dict(zip(names, rest))
        before_ref, high_ref, low_ref, diag_ref, sep, part_var, mine, other = rest[len(names) : len(names) + 8]
        sums, minus, high, low, sems, *scratch = rest[len(names) + 8 :]
        core = where_ref[3]
        copies = [
            pltpu.make_async_copy(before_ref, sums, sems.at[0]),
            pltpu.make_async_copy(high_ref, high, sems.at[1]),
            pltpu.make_async_copy(low_ref, low, sems.at[2]),
        ]

        def meanwhile():
            for copy in copies:
                copy.start()
            copies[0].wait()

        pair_loop((6, 6), (8, 8), refs, table_ref, mask_ref, sums, meanwhile, *scratch)
        product = jnp.concatenate([sums[0], sums[1]], axis=0)
        minus[...] = -product
        put = pltpu.make_async_copy(minus, sep, sems.at[3])
        put.start()
        copies[1].wait()
        copies[2].wait()
        update = dot3((high[...], low[...]), split(product), ROWS)
        row = lax.broadcasted_iota(jnp.int32, (768, 768), 0)
        column = lax.broadcasted_iota(jnp.int32, (768, 768), 1)
        part_var[...] = diag_ref[...] + jnp.sum(jnp.where(row == column, update, 0.0), axis=0, keepdims=True)
        for zz in range(4):
            lower = update[zz * 192 : zz * 192 + 96]
            upper = update[zz * 192 + 96 : zz * 192 + 192]

            @pl.when(core == 0)
            def _():
                mine[zz] = lower
                other[zz] = upper

            @pl.when(core != 0)
            def _():
                mine[zz] = upper
                other[zz] = lower

        put.wait()

    return pl.pallas_call(
        body,
        out_shape=(shape(768, 768), shape(1, 768), shape(4, 96, 768), shape(4, 96, 768)),
        in_specs=[SMEM, SMEM, SMEM] + [HBM] * (len(names) + 3) + [VMEM],
        out_specs=(HBM, VMEM, VMEM, VMEM),
        scratch_shapes=[
            pltpu.VMEM((2, 384, 768), FULL),
            pltpu.VMEM((768, 768), FULL),
            pltpu.VMEM((768, 768), SHORT),
            pltpu.VMEM((768, 768), SHORT),
            pltpu.SemaphoreType.DMA((4,)),
        ]
        + buffers(),
        compiler_params=pltpu.CompilerParams(vmem_limit_bytes=60 << 20),
        cost_estimate=cost(6),
        name="last_products",
    )(where, mask, table, *pieces.values(), before, own_high, own_low, diag_here)


def local(sigma_top, coupling, child_inverse, tile_mask, obs_node, obs_noise):
    sub = lax.axis_index("sub")
    row = lax.axis_index("row")
    x, y, z, core = sub // 4, sub % 4, row // 2, row % 2
    way = 1 - 2 * core
    table, early = work_table(x, y, z, core, way)
    where = jnp.concatenate([jnp.stack([x, y, z, core, way, row]).astype(jnp.int32), early])
    mask = tile_mask[0]

    inverse = child_inverse[0]
    column = lax.broadcasted_iota(jnp.int32, (96, 768), 1)
    line = lax.broadcasted_iota(jnp.int32, (96, 768), 0) + row * 96
    diag_here = jnp.sum(jnp.where(column == line, inverse, 0.0), axis=0, keepdims=True)
    child = obs_node // 768
    far_x = (child // 4 - x) % 4
    far_y = (child % 4 - y) % 4
    index = (far_x * 4 + far_y) * 768 + obs_node % 768

    a = sigma_top[:384]
    b = sigma_top[384:]
    m = coupling[0].reshape(2, 384, 768)
    za = ring(m, "z", 1, "p1z")
    xm, ym = ring(a, "x", 1, "p1"), ring(b, "y", 1, "p1")
    xp, yp = ring(a, "x", -1, "p1"), ring(b, "y", -1, "p1")

    one = (xm, ym, xp, yp)
    x2, y2 = ring(after(xm, *one), "x", 1, "p2"), ring(after(ym, *one), "y", 1, "p2")
    sib = swap(after(m, *one), "p2s")

    two = (x2, y2, sib, za)
    empty = jnp.zeros((1, 384, 384), FULL)
    a0 = jnp.concatenate([a[None], xm[None], xp[None], empty]).at[3].set(x2)
    b0 = jnp.concatenate([b[None], ym[None], yp[None], empty]).at[3].set(y2)
    a1, b1 = ring(after(a0, *two), "y", 1, "p3"), ring(after(b0, *two), "x", 1, "p3")
    zb = ring(after(sib, *two), "z", 1, "p3z")

    three = (a1, b1, zb, table, where, diag_here, index)
    a2, b2 = ring(after(a0, *three), "y", -1, "p4"), ring(after(b0, *three), "x", -1, "p4")
    zc = ring(after(za, *three), "z", 1, "p4z")
    zs = swap(after(zb, *three), "p4s")
    zt = swap(after(za, *three), "p4s")
    pieces = dict(a0=a0, a1=a1, b0=b0, b1=b1, own=m, sib=sib, za=za, zb=zb, zs=zs, zt=zt)
    sums = early_products(where, mask, table, pieces)

    four = (a2, b2, zc, zs, zt, sums)
    a3, b3 = ring(after(a1, *four), "y", 1, "p5"), ring(after(b1, *four), "x", 1, "p5")
    zu = swap(after(zc, *four), "p5s")
    pieces.update(a2=a2, b2=b2, zc=zc, zu=zu)
    sums, own_high, own_low = middle_products(where, mask, table, pieces, sums)

    pieces.update(a3=a3, b3=b3)
    final = {name: pieces[name] for name in BLOCKS + ("a3", "b3")}
    sep, part_var, mine, other = last_products(where, mask, table, final, sums, own_high, own_low, diag_here)

    arrived = swap(other)
    part = after(part_var + swap(part_var), arrived)
    half_sum = mine + arrived
    along_z = send(part, dz=1), send(part, dz=-1), send(part, dz=2)
    part = part + along_z[0] + along_z[1] + along_z[2]
    toward = lambda dz: lax.dynamic_index_in_dim(half_sum, (z + dz) % 4, 0, False)
    block_here = inverse + (toward(0) + send(toward(1), dz=1) + send(toward(-1), dz=-1) + send(toward(2), dz=2))
    part = after(part, half_sum)
    by_y = jnp.concatenate([part, send(part, dy=-1), send(part, dy=2), send(part, dy=1)], axis=0)
    by_xy = jnp.stack([by_y, send(by_y, dx=-1), send(by_y, dx=2), send(by_y, dx=1)])
    loo_var = by_xy.reshape(-1)[index] + obs_noise
    return sep[None], block_here[None], loo_var


def solution(mesh):
    placed = (
        P("row", "sub"),
        P("sub", "row", None),
        P("sub", "row", None),
        P("sub", None),
        P(("sub", "row")),
        P(("sub", "row")),
    )
    return jax.shard_map(
        local,
        mesh=mesh,
        in_specs=placed,
        out_specs=(P("sub", "row", None), P("sub", "row", None), P(("sub", "row"))),
        check_vma=False,
    )
```

```python
import jax
import jax.numpy as jnp
from jax import lax
from jax.experimental import pallas as pl
from jax.experimental.pallas import tpu as pltpu
from jax.sharding import PartitionSpec as P

AXES = ("sub", "row")
SHORT = jnp.bfloat16
FULL = jnp.float32


def place(x, y, z, c):
    return (x % 4) * 32 + (y % 4) * 8 + (z % 4) * 2 + c % 2


def send(value, dx=0, dy=0, dz=0, dc=0, turn=False):
    pairs = []
    for x in range(4):
        for y in range(4):
            for z in range(4):
                for c in range(2):
                    way = -1 if turn and c else 1
                    pairs.append((place(x, y, z, c), place(x + way * dx, y + way * dy, z + way * dz, c + dc)))
    return lax.ppermute(value, AXES, pairs)


def ring(value, axis, step, name):
    with jax.named_scope(name):
        return send(value, turn=True, **{"d" + axis: step})


def swap(value, name="swap"):
    with jax.named_scope(name):
        return send(value, dc=1)


def after(value, *earlier):
    return lax.optimization_barrier((value,) + earlier)[0]


def split(value):
    high = value.astype(SHORT)
    low = (value - high.astype(FULL)).astype(SHORT)
    return high, low


def dot3(a, b, dims):
    a_high, a_low = a
    b_high, b_low = b
    one = lambda u, v: lax.dot_general(u, v, (dims, ((), ())), preferred_element_type=FULL)
    return one(a_high, b_high) + (one(a_low, b_high) + one(a_high, b_low))


ROWS = ((1,), (0,))

LINES = ("a0", "a1", "a2", "a3", "b0", "b1", "b2", "b3")
BLOCKS = ("own", "sib", "za", "zb", "zc", "zu", "zs", "zt")


def work_table(x, y, z, core, way):
    unit = jnp.arange(32, dtype=jnp.int32)
    group, line, spot = unit // 16, unit // 4 % 4, unit % 4
    step = lambda k: jnp.where(k == 3, 2, jnp.where(k == 0, 0, 2 * k - 3))
    x_step = jnp.where(group == 0, step(spot), step(line))
    y_step = jnp.where(group == 0, step(line), step(spot))
    at_x = (x + way * x_step) & 3
    at_y = (y + way * y_step) & 3
    far = ((z - at_x) * way) & 3
    half = (far * 2 + ((at_y >> 1) ^ core)) * 2 + (at_y & 1)
    rank = jnp.where(line == 3, 2, jnp.where((line == 2) | (far == 2), 1, 0))
    early = jnp.sum((rank.reshape(2, 16) == 0).astype(jnp.int32), axis=1)
    key = (group * 3 + rank) * 32 + unit
    order = jnp.sum((key[None, :] < key[:, None]).astype(jnp.int32), axis=1)
    here = (order[None, :] == unit[:, None]).astype(jnp.int32)
    pick = lambda v: jnp.sum(here * v[None, :], axis=1)
    return jnp.stack([pick(unit), pick(half), pick(at_x * 4 + at_y)]), early


def pair_loop(begin, end, refs, table, mask, sums, meanwhile, s_buf, m_buf, spot, s_sem, m_sem):
    slots = s_buf.shape[0]
    first_group = end[0] - begin[0]
    count = first_group + end[1] - begin[1]

    def start(q, slot):
        group = jnp.where(q < first_group, 0, 1)
        pair = jnp.where(q < first_group, begin[0] + q, begin[1] + q - first_group)
        spot[slot, 2] = group
        for part in range(2):
            entry = group * 16 + pair * 2 + part
            unit = table[0, entry]
            half = table[1, entry]
            spot[slot, part] = table[2, entry]
            s_target = s_buf.at[slot, :, pl.ds(part * 384, 384)]
            m_target = m_buf.at[slot, pl.ds(part * 384, 384), :]
            for number, name in enumerate(LINES):
                if name in refs:

                    @pl.when(unit >> 2 == number)
                    def _():
                        pltpu.make_async_copy(refs[name].at[unit & 3], s_target, s_sem.at[slot, part]).start()

            for number, name in enumerate(BLOCKS):
                if name in refs:

                    @pl.when(half >> 1 == number)
                    def _():
                        pltpu.make_async_copy(refs[name].at[half & 1], m_target, m_sem.at[slot, part]).start()

    def finish(slot):
        for part in range(2):
            target = s_buf.at[slot, :, pl.ds(part * 384, 384)]
            pltpu.make_async_copy(refs["b0" if "b0" in refs else "b3"].at[0], target, s_sem.at[slot, part]).wait()
            target = m_buf.at[slot, pl.ds(part * 384, 384), :]
            pltpu.make_async_copy(refs["own"].at[0], target, m_sem.at[slot, part]).wait()
        pieces = []
        for part in range(2):
            block = spot[slot, part]
            for third in range(3):
                factor = mask[(block * 3 + third) >> 1].astype(FULL)
                pieces.append(m_buf[slot, pl.ds(part * 384 + third * 128, 128), :] * factor)
        part_sum = dot3(split(s_buf[slot]), split(jnp.concatenate(pieces, axis=0)), ROWS)
        group = spot[slot, 2]
        sums[group] = sums[group] + part_sum

    for ahead in range(slots - 1):

        @pl.when(ahead < count)
        def _():
            start(ahead, ahead)

    if meanwhile is not None:
        meanwhile()

    def step(p, carry):
        later = p + slots - 1

        @pl.when(later < count)
        def _():
            start(later, lax.rem(later, slots))

        finish(lax.rem(p, slots))
        return carry

    lax.fori_loop(0, count, step, 0)


HBM = pl.BlockSpec(memory_space=pl.ANY)
SMEM = pl.BlockSpec(memory_space=pltpu.SMEM)
VMEM = pl.BlockSpec(memory_space=pltpu.VMEM)


def buffers(slots=3):
    return [
        pltpu.VMEM((slots, 384, 768), FULL),
        pltpu.VMEM((slots, 768, 768), FULL),
        pltpu.SMEM((slots, 3), jnp.int32),
        pltpu.SemaphoreType.DMA((slots, 2)),
        pltpu.SemaphoreType.DMA((slots, 2)),
    ]


def shape(*dims):
    return jax.ShapeDtypeStruct(dims, FULL)


def cost(pairs):
    return pl.CostEstimate(flops=1_400_000_000 * pairs, bytes_accessed=3_600_000 * pairs, transcendentals=0)


def early_products(where, mask, table, pieces):
    names = list(pieces)

    def body(where_ref, mask_ref, table_ref, *rest):
        refs = dict(zip(names, rest))
        sums, *scratch = rest[len(names) :]

        def meanwhile():
            sums[...] = jnp.zeros_like(sums)

        end = (where_ref[6] // 2, where_ref[7] // 2)
        pair_loop((0, 0), end, refs, table_ref, mask_ref, sums, meanwhile, *scratch)

    return pl.pallas_call(
        body,
        out_shape=shape(2, 384, 768),
        in_specs=[SMEM, SMEM, SMEM] + [HBM] * len(names),
        out_specs=VMEM,
        scratch_shapes=buffers(),
        compiler_params=pltpu.CompilerParams(vmem_limit_bytes=60 << 20),
        cost_estimate=cost(6),
        name="early_products",
    )(where, mask, table, *pieces.values())


def middle_products(where, mask, table, pieces, before):
    names = list(pieces)

    def body(where_ref, mask_ref, table_ref, *rest):
        refs = dict(zip(names, rest))
        before_ref, own_ref, sums, own_high, own_low, sem, *scratch = rest[len(names) :]
        copy = pltpu.make_async_copy(before_ref, sums, sem)
        copy.start()

        def meanwhile():
            row = where_ref[5]
            tiles = [
                mask_ref[row * 3 + k].astype(FULL) * own_ref[pl.ds(k * 256, 256), :] for k in range(3)
            ]
            high, low = split(jnp.concatenate(tiles, axis=0).T)
            own_high[...] = high
            own_low[...] = low
            copy.wait()

        early = (where_ref[6] // 2, where_ref[7] // 2)
        pair_loop(early, (6, 6), refs, table_ref, mask_ref, sums, meanwhile, *scratch)

    half = jax.ShapeDtypeStruct((768, 768), SHORT)
    return pl.pallas_call(
        body,
        out_shape=(shape(2, 384, 768), half, half),
        in_specs=[SMEM, SMEM, SMEM] + [HBM] * (len(names) + 1) + [VMEM],
        out_specs=(VMEM, VMEM, VMEM),
        scratch_shapes=[pltpu.SemaphoreType.DMA] + buffers(),
        compiler_params=pltpu.CompilerParams(vmem_limit_bytes=60 << 20),
        cost_estimate=cost(6),
        name="middle_products",
    )(where, mask, table, *pieces.values(), before, pieces["own"].reshape(768, 768))


def last_products(where, mask, table, pieces, before, own_high, own_low, diag_here):
    names = list(pieces)

    def body(where_ref, mask_ref, table_ref, *rest):
        refs = dict(zip(names, rest))
        before_ref, high_ref, low_ref, diag_ref, sep, part_var, mine, other = rest[len(names) : len(names) + 8]
        sums, minus, high, low, sems, *scratch = rest[len(names) + 8 :]
        core = where_ref[3]
        copies = [
            pltpu.make_async_copy(before_ref, sums, sems.at[0]),
            pltpu.make_async_copy(high_ref, high, sems.at[1]),
            pltpu.make_async_copy(low_ref, low, sems.at[2]),
        ]

        def meanwhile():
            for copy in copies:
                copy.start()
            copies[0].wait()

        pair_loop((6, 6), (8, 8), refs, table_ref, mask_ref, sums, meanwhile, *scratch)
        product = jnp.concatenate([sums[0], sums[1]], axis=0)
        minus[...] = -product
        put = pltpu.make_async_copy(minus, sep, sems.at[3])
        put.start()
        copies[1].wait()
        copies[2].wait()
        update = dot3((high[...], low[...]), split(product), ROWS)
        row = lax.broadcasted_iota(jnp.int32, (768, 768), 0)
        column = lax.broadcasted_iota(jnp.int32, (768, 768), 1)
        part_var[...] = diag_ref[...] + jnp.sum(jnp.where(row == column, update, 0.0), axis=0, keepdims=True)
        for zz in range(4):
            lower = update[zz * 192 : zz * 192 + 96]
            upper = update[zz * 192 + 96 : zz * 192 + 192]

            @pl.when(core == 0)
            def _():
                mine[zz] = lower
                other[zz] = upper

            @pl.when(core != 0)
            def _():
                mine[zz] = upper
                other[zz] = lower

        put.wait()

    return pl.pallas_call(
        body,
        out_shape=(shape(768, 768), shape(1, 768), shape(4, 96, 768), shape(4, 96, 768)),
        in_specs=[SMEM, SMEM, SMEM] + [HBM] * (len(names) + 3) + [VMEM],
        out_specs=(HBM, VMEM, VMEM, VMEM),
        scratch_shapes=[
            pltpu.VMEM((2, 384, 768), FULL),
            pltpu.VMEM((768, 768), FULL),
            pltpu.VMEM((768, 768), SHORT),
            pltpu.VMEM((768, 768), SHORT),
            pltpu.SemaphoreType.DMA((4,)),
        ]
        + buffers(2),
        compiler_params=pltpu.CompilerParams(vmem_limit_bytes=60 << 20),
        cost_estimate=cost(6),
        name="last_products",
    )(where, mask, table, *pieces.values(), before, own_high, own_low, diag_here)


def local(sigma_top, coupling, child_inverse, tile_mask, obs_node, obs_noise):
    sub = lax.axis_index("sub")
    row = lax.axis_index("row")
    x, y, z, core = sub // 4, sub % 4, row // 2, row % 2
    way = 1 - 2 * core
    table, early = work_table(x, y, z, core, way)
    where = jnp.concatenate([jnp.stack([x, y, z, core, way, row]).astype(jnp.int32), early])
    mask = tile_mask[0]

    inverse = child_inverse[0]
    column = lax.broadcasted_iota(jnp.int32, (96, 768), 1)
    line = lax.broadcasted_iota(jnp.int32, (96, 768), 0) + row * 96
    diag_here = jnp.sum(jnp.where(column == line, inverse, 0.0), axis=0, keepdims=True)
    child = obs_node // 768
    far_x = (child // 4 - x) % 4
    far_y = (child % 4 - y) % 4
    index = (far_x * 4 + far_y) * 768 + obs_node % 768

    a = sigma_top[:384]
    b = sigma_top[384:]
    m = coupling[0].reshape(2, 384, 768)
    za = ring(m, "z", 1, "p1z")
    xm, ym = ring(a, "x", 1, "p1"), ring(b, "y", 1, "p1")
    xp, yp = ring(a, "x", -1, "p1"), ring(b, "y", -1, "p1")

    one = (xm, ym, xp, yp)
    x2, y2 = ring(after(xm, *one), "x", 1, "p2"), ring(after(ym, *one), "y", 1, "p2")
    sib = swap(after(m, *one), "p2s")

    two = (x2, y2, sib, za)
    empty = jnp.zeros((1, 384, 384), FULL)
    a0 = jnp.concatenate([a[None], xm[None], xp[None], empty]).at[3].set(x2)
    b0 = jnp.concatenate([b[None], ym[None], yp[None], empty]).at[3].set(y2)
    a1, b1 = ring(after(a0, *two), "y", 1, "p3"), ring(after(b0, *two), "x", 1, "p3")
    zb = ring(after(sib, *two), "z", 1, "p3z")

    three = (a1, b1, zb, table, where, diag_here, index)
    a2, b2 = ring(after(a0, *three), "y", -1, "p4"), ring(after(b0, *three), "x", -1, "p4")
    zc = ring(after(za, *three), "z", 1, "p4z")
    zs = swap(after(zb, *three), "p4s")
    zt = swap(after(za, *three), "p4s")
    pieces = dict(a0=a0, a1=a1, b0=b0, b1=b1, own=m, sib=sib, za=za, zb=zb, zs=zs, zt=zt)
    sums = early_products(where, mask, table, pieces)

    four = (a2, b2, zc, zs, zt, sums)
    a3, b3 = ring(after(a1, *four), "y", 1, "p5"), ring(after(b1, *four), "x", 1, "p5")
    zu = swap(after(zc, *four), "p5s")
    pieces.update(a2=a2, b2=b2, zc=zc, zu=zu)
    sums, own_high, own_low = middle_products(where, mask, table, pieces, sums)

    pieces.update(a3=a3, b3=b3)
    final = {name: pieces[name] for name in BLOCKS + ("a3", "b3")}
    sep, part_var, mine, other = last_products(where, mask, table, final, sums, own_high, own_low, diag_here)

    arrived = swap(other)
    part = after(part_var + swap(part_var), arrived)
    half_sum = mine + arrived
    along_z = send(part, dz=1), send(part, dz=-1), send(part, dz=2)
    part = part + along_z[0] + along_z[1] + along_z[2]
    toward = lambda dz: lax.dynamic_index_in_dim(half_sum, (z + dz) % 4, 0, False)
    block_here = inverse + (toward(0) + send(toward(1), dz=1) + send(toward(-1), dz=-1) + send(toward(2), dz=2))
    part = after(part, half_sum)
    by_y = jnp.concatenate([part, send(part, dy=-1), send(part, dy=2), send(part, dy=1)], axis=0)
    by_xy = jnp.stack([by_y, send(by_y, dx=-1), send(by_y, dx=2), send(by_y, dx=1)])
    loo_var = by_xy.reshape(-1)[index] + obs_noise
    return sep[None], block_here[None], loo_var


def solution(mesh):
    placed = (
        P("row", "sub"),
        P("sub", "row", None),
        P("sub", "row", None),
        P("sub", None),
        P(("sub", "row")),
        P(("sub", "row")),
    )
    return jax.shard_map(
        local,
        mesh=mesh,
        in_specs=placed,
        out_specs=(P("sub", "row", None), P("sub", "row", None), P(("sub", "row"))),
        check_vma=False,
    )
```
